32 devices in a mesh: dp: 4 (over y, core), mp: 8 (over z, x).
Axes of the slice: x: 2, y: 2, z: 4, core: 2. Of those that a mesh axis runs over, the one named last changes fastest.
Arguments:
- pair_tokens: bfloat16 [64, 48, 8192], P('dp', None, 'mp'), may hold values from -6 to 6
- norm_gain: float32 [8192], replicated, may hold values from 0.1 to 1.9
- q_weight: bfloat16 [8192, 4096], P('dp', 'mp'), may hold values from -1.5 to 1.5
- k_weight: bfloat16 [8192, 1024], P('dp', 'mp'), may hold values from -1.5 to 1.5
- value_weight: bfloat16 [8192, 1024], P('dp', 'mp'), may hold values from -0.0625 to 0.0625
- o_weight: bfloat16 [4096, 8192], P('mp', 'dp'), may hold values from -0.375 to 0.375
- pair_row: int32 [64], replicated, may hold values from 0 to 15, as said below
- pair_span: int32 [64, 2], replicated, may hold values from 0 to 128, as said below
- block_ids: int32 [2048], P('dp'), may hold values from 0 to 11, as said below
Outputs:
- attn_out: bfloat16 [2048, 8192], P('dp', 'mp')
The draws below stay inside these ranges and needn't reach their ends.
Inputs may be any that keep to these rules, and one draw needn't show every extreme that they name: `pair_row`: every packed row is tiled exactly by the spans of the pairs that name it; the pairs listed on one index of dp that name rows of one index of dp number at most 4, and 4 is reached. `pair_span`: each span holds one pair, start before end; end - start is at least 3 and at most 48; 48 is reached in every row, and the last pair of every row ends at 128. `block_ids`: the pair's place counts the pairs of its row in order of position; roles are 0 prompt, 1 chosen, 2 rejected, in that order within each pair, each present; consistent with pair_row and pair_span.
All inputs are finite; a program needn't handle non-finite values.
Results may differ from the reference program's by a relative error of at most 0.013.
Values may be sent and summed in bfloat16 or wider, within the bound.
A program may use at most 128 MiB of HBM per device.

```python
import jax
import jax.numpy as jnp
from jax import lax

MODEL_WIDTH = 8192
QUERY_HEADS = 32
KEY_VALUE_HEADS = 8
HEAD_SIZE = 128
ROW_TOKENS = 128
PAIR_CAP = 48
PAIRS_ROW = 4
PACK_ROWS = 4
QUERY_PER_KV = 4
ROWS = 16
TOKENS = 2048
PAIRS_DEV = 16
NPAIRS = 64
N_DP = 4
N_MP = 8


def packing_layout(key):
    key_rows = jax.random.split(jax.random.fold_in(key, 7), 7)
    count = PAIRS_ROW
    rest = ROW_TOKENS - PAIR_CAP
    shortest = rest // 4
    spare = rest - (count - 1) * shortest
    cuts = jnp.sort(jax.random.randint(key_rows[0], (ROWS, count - 2), 0, spare + 1), axis=1)
    edges = jnp.concatenate([jnp.zeros((ROWS, 1), jnp.int32), cuts, jnp.full((ROWS, 1), spare, jnp.int32)], axis=1)
    others = edges[:, 1:] - edges[:, :-1] + shortest
    unordered = jnp.concatenate([jnp.full((ROWS, 1), PAIR_CAP, jnp.int32), others], axis=1)
    order_keys = jax.random.randint(key_rows[1], (ROWS, count), 0, 1 << 20) * count + jnp.arange(count)
    order = jnp.argsort(order_keys, axis=1)
    lengths = jnp.take_along_axis(unordered, order, axis=1)
    starts = jnp.cumsum(lengths, axis=1) - lengths
    prompt = 1 + jax.random.randint(key_rows[2], (ROWS, count), 0, lengths - 2)
    chosen = 1 + jax.random.randint(key_rows[3], (ROWS, count), 0, lengths - 1 - prompt)
    placing = jax.random.permutation(key_rows[4], N_DP)
    shift_all = jax.random.permutation(key_rows[5], N_DP)
    shifts = shift_all[jnp.arange(PAIRS_DEV) % N_DP]
    slot_keys = jax.random.randint(key_rows[6], (N_DP, PAIRS_DEV), 0, 1 << 20) * PAIRS_DEV + jnp.arange(PAIRS_DEV)[None, :]
    slot_of = jnp.argsort(slot_keys, axis=1)
    source = jnp.arange(NPAIRS) // PAIRS_DEV
    within_src = jnp.arange(NPAIRS) % PAIRS_DEV
    owner = (placing[source] + shifts[within_src]) % N_DP
    slot = slot_of[owner, within_src]
    row = owner * PACK_ROWS + slot // count
    place = slot % count
    return (row, starts, lengths, prompt, chosen, place)


def draw_pair_row(key, part):
    row, starts, lengths, prompt, chosen, place = packing_layout(key)
    return row.astype(jnp.int32)


def draw_pair_span(key, part):
    row, starts, lengths, prompt, chosen, place = packing_layout(key)
    first = starts[row, place]
    return jnp.stack([first, first + lengths[row, place]], axis=1).astype(jnp.int32)


def draw_block_ids(key, part):
    row, starts, lengths, prompt, chosen, place = packing_layout(key)
    steps_t = jnp.arange(ROW_TOKENS)
    which = jnp.sum((steps_t[None, :, None] >= starts[:, None, 1:]).astype(jnp.int32), axis=2)
    offset = steps_t[None, :] - jnp.take_along_axis(starts, which, axis=1)
    prompt_len = jnp.take_along_axis(prompt, which, axis=1)
    chosen_len = jnp.take_along_axis(chosen, which, axis=1)
    role = (offset >= prompt_len).astype(jnp.int32) + (offset >= prompt_len + chosen_len).astype(jnp.int32)
    return (3 * which + role).reshape(-1).astype(jnp.int32)


def projections(key):
    key_rows = jax.random.split(jax.random.fold_in(key, 11), 2)
    rotary_base = jnp.clip(jax.random.normal(key_rows[0], (MODEL_WIDTH, KEY_VALUE_HEADS * HEAD_SIZE), jnp.float32), -4.0, 4.0) * MODEL_WIDTH ** (-0.5)
    noise = jnp.clip(jax.random.normal(key_rows[1], (MODEL_WIDTH, QUERY_HEADS * HEAD_SIZE), jnp.float32), -4.0, 4.0) * MODEL_WIDTH ** (-0.5)
    return (rotary_base, noise)


def draw_k_weight(key, part):
    rotary_base, noise = projections(key)
    return rotary_base.astype(jnp.bfloat16)


def draw_q_weight(key, part):
    rotary_base, noise = projections(key)
    return noise.astype(jnp.bfloat16)


def block_scale(rng, shape, cuts, least, high):
    loudness = 1.0
    for dim, blocks in cuts:
        heights = jax.random.uniform(jax.random.fold_in(jax.random.fold_in(rng, 6), dim), (blocks,), jnp.float32, least / len(cuts), high / len(cuts))
        loudness = loudness * jnp.repeat(jnp.exp(heights), shape[dim] // blocks).reshape((-1,) + (1,) * (len(shape) - 1 - dim))
    return loudness


def normal_values(rng, extent, deviation, limit, pieces=(), kind=jnp.bfloat16):
    gain = block_scale(rng, extent, pieces, -0.22, 0.18) if pieces else 1.0
    values = jax.random.normal(rng, extent, jnp.float32) * deviation * gain
    return jnp.minimum(jnp.maximum(values, -limit), limit).astype(kind)


def setup_inputs(seed: int = 0) -> dict:
    key_of = jax.random.split(jax.random.key(seed), 10)
    return {
        "pair_tokens": normal_values(key_of[0], (NPAIRS, PAIR_CAP, MODEL_WIDTH), 1.0, 6.0, ((0, 4), (2, 8))),
        "norm_gain": jnp.clip(1.0 + 0.18 * jax.random.normal(key_of[1], (MODEL_WIDTH,), jnp.float32), 0.1, 1.9),
        "q_weight": draw_q_weight(jax.random.fold_in(key_of[9], 71), 0),
        "k_weight": draw_k_weight(jax.random.fold_in(key_of[9], 71), 0),
        "value_weight": normal_values(key_of[4], (MODEL_WIDTH, KEY_VALUE_HEADS * HEAD_SIZE), MODEL_WIDTH ** -0.5, 0.0625, ((0, 4), (1, 8))),
        "o_weight": normal_values(key_of[5], (QUERY_HEADS * HEAD_SIZE, MODEL_WIDTH), (QUERY_HEADS * HEAD_SIZE // 16) ** -0.5, 0.375, ((0, 8), (1, 4))),
        "pair_row": draw_pair_row(jax.random.fold_in(key_of[9], 71), 0),
        "pair_span": draw_pair_span(jax.random.fold_in(key_of[9], 71), 0),
        "block_ids": draw_block_ids(jax.random.fold_in(key_of[9], 71), 0),
    }


def apply_rotary(values, token_position, heads):
    half = HEAD_SIZE // 2
    freq = 500000.0 ** (-(jnp.arange(half, dtype=jnp.float32) * 2.0 / HEAD_SIZE))
    angle = token_position.astype(jnp.float32)[:, None] * freq[None, :]
    cosine = jnp.cos(angle)[:, None, :]
    sine = jnp.sin(angle)[:, None, :]
    shaped = values.reshape(values.shape[0], heads, HEAD_SIZE)
    first = shaped[..., :half]
    second = shaped[..., half:]
    turned = jnp.concatenate([first * cosine - second * sine, second * cosine + first * sine], axis=-1)
    return turned.reshape(values.shape[0], heads * HEAD_SIZE).astype(jnp.bfloat16)

def row_mask(ids):
    pair_of = ids // 3
    role_of = ids % 3
    steps_a = jnp.arange(ids.shape[0])
    causal = steps_a[None, :] <= steps_a[:, None]
    same = pair_of[:, None] == pair_of[None, :]
    hidden_pair = (role_of[:, None] == 2) & (role_of[None, :] == 1)
    return causal & same & jnp.logical_not(hidden_pair)

def reference(pair_tokens, norm_gain, q_weight, k_weight, value_weight, o_weight, pair_row, pair_span, block_ids):
    slots = jnp.arange(PAIR_CAP, dtype=jnp.int32)
    length = pair_span[:, 1] - pair_span[:, 0]
    target = pair_row[:, None] * ROW_TOKENS + pair_span[:, 0][:, None] + slots[None, :]
    target = jnp.where(slots[None, :] < length[:, None], target, TOKENS).astype(jnp.int32)
    packed = jnp.zeros((TOKENS, MODEL_WIDTH), jnp.bfloat16).at[target.reshape(-1)].set(pair_tokens.reshape(-1, MODEL_WIDTH), mode='drop')
    group_width = QUERY_HEADS * HEAD_SIZE // N_MP

    def one_row(inputs):
        row_tokens, ids = inputs
        visible = row_mask(ids)
        token_position = lax.optimization_barrier(jnp.sum(visible.astype(jnp.int32), axis=1)) - 1
        wide = row_tokens.astype(jnp.float32)
        scale = lax.rsqrt(lax.optimization_barrier(jnp.mean(wide * wide, axis=-1, keepdims=True)) + 1e-05)
        normed = (wide * scale * norm_gain[None, :]).astype(jnp.bfloat16)
        query_heads = jnp.dot(normed, q_weight, preferred_element_type=jnp.float32)
        key_rows = jnp.dot(normed, k_weight, preferred_element_type=jnp.float32)
        value_heads = jnp.dot(normed, value_weight, preferred_element_type=jnp.float32).astype(jnp.bfloat16)
        rotated_query = apply_rotary(query_heads, token_position, QUERY_HEADS).astype(jnp.float32).reshape(ROW_TOKENS, KEY_VALUE_HEADS, QUERY_PER_KV, HEAD_SIZE)
        rotated_key = apply_rotary(key_rows, token_position, KEY_VALUE_HEADS).astype(jnp.float32).reshape(ROW_TOKENS, KEY_VALUE_HEADS, HEAD_SIZE)
        value_expanded = value_heads.astype(jnp.float32).reshape(ROW_TOKENS, KEY_VALUE_HEADS, HEAD_SIZE)
        scores = jnp.einsum('ihgd,jhd->hgij', rotated_query, rotated_key) * HEAD_SIZE ** (-0.5)
        scores = jnp.where(visible[None, None], scores, -1e+30)
        top = lax.optimization_barrier(jnp.max(scores, axis=-1, keepdims=True))
        expo = jnp.exp(scores - top)
        probs = (expo / lax.optimization_barrier(jnp.sum(expo, axis=-1, keepdims=True))).astype(jnp.bfloat16)
        attn = jnp.einsum('hgij,jhd->ihgd', probs.astype(jnp.float32), value_expanded).astype(jnp.bfloat16)
        attn = attn.reshape(ROW_TOKENS, QUERY_HEADS * HEAD_SIZE)
        total = jnp.zeros((ROW_TOKENS, MODEL_WIDTH), jnp.float32)
        for group in range(N_MP):
            part = jnp.dot(attn[:, group * group_width:(group + 1) * group_width], o_weight[group * group_width:(group + 1) * group_width], preferred_element_type=jnp.float32).astype(jnp.bfloat16)
            part = lax.optimization_barrier(part)
            total = total + part.astype(jnp.float32)
        return total.astype(jnp.bfloat16)
    result = lax.map(one_row, (packed.reshape(ROWS, ROW_TOKENS, MODEL_WIDTH), block_ids.reshape(ROWS, ROW_TOKENS)))
    return result.reshape(TOKENS, MODEL_WIDTH)
```

```python
import functools

import jax
import jax.numpy as jnp
from jax import lax
from jax.experimental import pallas as pl
from jax.experimental.pallas import tpu as pltpu
from jax.sharding import PartitionSpec as P

HEAD_SIZE = 128
ROW_TOKENS = 128
QUERY_PER_KV = 4
PIECES = 2
MESH = pl.DeviceIdType.MESH


def row_mask(ids):
    pair_of = ids // 3
    role_of = ids % 3
    steps_a = jnp.arange(ids.shape[0])
    causal = steps_a[None, :] <= steps_a[:, None]
    same = pair_of[:, None] == pair_of[None, :]
    hidden_pair = (role_of[:, None] == 2) & (role_of[None, :] == 1)
    return causal & same & jnp.logical_not(hidden_pair)


def ring_member(place, count):
    place = lax.rem(place + 2 * count, count)
    return jnp.where(place < count // 2, 2 * place, 2 * (count - 1 - place) + 1)


def kernel(
    n_dp, n_mp,
    x_ref, gain_ref, q_ref, k_ref, v_ref, o_ref, cos_ref, sin_ref, vis_ref,
    out_ref,
    xg, wq, wk, wv, wo, acc, attn, sums, terms,
    own_sem, w_send, w_recv, x_send, x_recv, s_send, s_recv,
):
    me_dp = lax.axis_index("dp")
    me_mp = lax.axis_index("mp")
    place = jnp.where(lax.rem(me_mp, 2) == 0, me_mp // 2, n_mp - 1 - me_mp // 2)
    sides = (ring_member(place + 1, n_mp), ring_member(place - 1, n_mp))
    groups = n_dp // 2
    core = lax.rem(me_dp, 2)
    partner = me_dp + 1 - 2 * core
    others = [lax.rem(me_dp + 2 * j, n_dp) for j in range(1, groups)]
    tokens, chunk = x_ref.shape
    half = tokens // 2
    piece = half // PIECES

    barrier = pltpu.get_barrier_semaphore()
    for side in sides:
        pl.semaphore_signal(barrier, inc=1, device_id={"mp": side}, device_id_type=MESH)
    for peer in [partner] + others:
        pl.semaphore_signal(barrier, inc=1, device_id={"dp": peer}, device_id_type=MESH)
    pl.semaphore_wait(barrier, 2 + 1 + len(others))

    def part(which, owner):
        if which == 3:
            width = o_ref.shape[1]
            return wo.at[:, pl.ds(pl.multiple_of(owner * width, 128), width)]
        full = (wq, wk, wv)[which]
        depth = q_ref.shape[0]
        return full.at[pl.ds(pl.multiple_of(owner * depth, 16), depth), :]

    shards = (q_ref, k_ref, v_ref, o_ref)

    def weight_copy(which, owner, source, slot, peer):
        return pltpu.make_async_remote_copy(
            src_ref=source,
            dst_ref=part(which, owner),
            send_sem=w_send.at[which, slot],
            recv_sem=w_recv.at[which, owner],
            device_id={"dp": peer},
            device_id_type=MESH,
        )

    def x_copy(step, way, sub):
        sign = -1 if way == 0 else 1
        chunk_of = ring_member(place + sign * step, n_mp)
        rows = pl.ds(way * half + sub * piece, piece)
        ref = xg.at[chunk_of, rows, :]
        return pltpu.make_async_remote_copy(
            src_ref=ref,
            dst_ref=ref,
            send_sem=x_send.at[way, sub, step],
            recv_sem=x_recv.at[way, sub, step],
            device_id={"mp": sides[way]},
            device_id_type=MESH,
        )

    def x_arrival(step, way, sub):
        sign = -1 if way == 0 else 1
        chunk_of = ring_member(place + sign * (step + 1), n_mp)
        rows = pl.ds(way * half + sub * piece, piece)
        ref = xg.at[chunk_of, rows, :]
        return pltpu.make_async_remote_copy(
            src_ref=ref,
            dst_ref=ref,
            send_sem=x_send.at[way, sub, step],
            recv_sem=x_recv.at[way, sub, step],
            device_id={"mp": sides[way]},
            device_id_type=MESH,
        )

    own_x = pltpu.make_async_copy(x_ref, xg.at[me_mp], own_sem.at[4])
    own_x.start()
    owns = [
        pltpu.make_async_copy(shards[w], part(w, me_dp), own_sem.at[w]) for w in range(4)
    ]
    for w in range(4):
        for j, peer in enumerate(others):
            weight_copy(w, me_dp, shards[w], 1 + j, peer).start()
    own_x.wait()
    for sub in range(PIECES):
        for way in range(2):
            x_copy(0, way, sub).start()
    for w in range(4):
        owns[w].start()
        weight_copy(w, me_dp, shards[w], 0, partner).start()

    def pass_weight(w):
        for j in range(1, groups):
            owner = lax.rem(me_dp + n_dp - 2 * j, n_dp)
            weight_copy(w, owner, part(w, owner), 0, partner).wait_recv()
            weight_copy(w, owner, part(w, owner), groups + j - 1, partner).start()

    def weight_done(w):
        owns[w].wait()
        for i in range(groups):
            owner = lax.rem(partner + 2 * i, n_dp)
            weight_copy(w, owner, part(w, owner), 0, partner).wait_recv()

    def gather_step(step, carry):
        for sub in range(PIECES):
            for way in range(2):
                x_arrival(step, way, sub).wait_recv()
                x_copy(step + 1, way, sub).start()
        return carry

    late = max(n_mp - 3, 0)
    lax.fori_loop(0, late, gather_step, 0)
    pass_weight(0)
    lax.fori_loop(late, n_mp - 2, gather_step, 0)
    pass_weight(1)
    pass_weight(2)
    for sub in range(PIECES):
        for way in range(2):
            x_arrival(n_mp - 2, way, sub).wait_recv()
    for w in range(3):
        weight_done(w)

    q_width = wq.shape[1]
    k_width = wk.shape[1]
    acc[...] = jnp.zeros_like(acc)

    def project(g, squares):
        wide = xg[g].astype(jnp.float32)
        squares = squares + jnp.sum(wide * wide, axis=1, keepdims=True)
        scaled = (wide * gain_ref[pl.ds(g, 1), :]).astype(jnp.bfloat16)
        rows = pl.ds(pl.multiple_of(g * chunk, 16), chunk)
        acc[:, 0:q_width] += jnp.dot(scaled, wq[rows, :], preferred_element_type=jnp.float32)
        acc[:, q_width:q_width + k_width] += jnp.dot(
            scaled, wk[rows, :], preferred_element_type=jnp.float32
        )
        acc[:, q_width + k_width:] += jnp.dot(
            scaled, wv[rows, :], preferred_element_type=jnp.float32
        )
        return squares

    squares = lax.fori_loop(0, n_mp, project, jnp.zeros((tokens, 1), jnp.float32))
    acc[...] = acc[...] * lax.rsqrt(squares / (n_mp * chunk) + 1e-05)

    def turn(u, cosine, sine):
        return (u * cosine + pltpu.roll(u, HEAD_SIZE // 2, 1) * sine).astype(jnp.bfloat16)

    def attend(r, carry):
        rows = pl.ds(pl.multiple_of(r * ROW_TOKENS, ROW_TOKENS), ROW_TOKENS)
        cosine = cos_ref[rows, :]
        sine = sin_ref[rows, :]
        seen = vis_ref[rows, :] > 0
        for kv in range(k_width // HEAD_SIZE):
            at_k = q_width + kv * HEAD_SIZE
            key = turn(acc[rows, at_k:at_k + HEAD_SIZE], cosine, sine)
            value = acc[rows, at_k + k_width:at_k + k_width + HEAD_SIZE].astype(jnp.bfloat16)
            for h in range(kv * QUERY_PER_KV, (kv + 1) * QUERY_PER_KV):
                at = slice(h * HEAD_SIZE, (h + 1) * HEAD_SIZE)
                query = turn(acc[rows, at], cosine, sine)
                scores = lax.dot_general(
                    query, key, (((1,), (1,)), ((), ())), preferred_element_type=jnp.float32
                ) * HEAD_SIZE ** (-0.5)
                scores = jnp.where(seen, scores, -1e30)
                expo = jnp.exp(scores - jnp.max(scores, axis=-1, keepdims=True))
                probs = (expo / jnp.sum(expo, axis=-1, keepdims=True)).astype(jnp.bfloat16)
                attn[rows, at] = jnp.dot(
                    probs, value, preferred_element_type=jnp.float32
                ).astype(jnp.bfloat16)
        return carry

    lax.fori_loop(0, tokens // ROW_TOKENS, attend, 0)
    pass_weight(3)
    weight_done(3)

    def make_terms(hop):
        for way in range(2):
            sign = -1 if way == 0 else 1
            g = ring_member(place + sign * hop, n_mp)
            columns = pl.ds(pl.multiple_of(g * chunk, 128), chunk)
            terms[way] = jnp.dot(
                attn[way * half:(way + 1) * half, :],
                wo[:, columns],
                preferred_element_type=jnp.float32,
            )

    def sum_copy(slot, way, sub):
        rows = pl.ds(sub * piece, piece)
        return pltpu.make_async_remote_copy(
            src_ref=sums.at[way, slot, rows, :],
            dst_ref=sums.at[way, slot + 1, rows, :],
            send_sem=s_send.at[way, sub, slot],
            recv_sem=s_recv.at[way, sub, slot],
            device_id={"mp": sides[way]},
            device_id_type=MESH,
        )

    make_terms(1)
    for sub in range(PIECES):
        for way in range(2):
            rows = slice(sub * piece, (sub + 1) * piece)
            sums[way, 0, rows, :] = terms[way, rows, :].astype(jnp.bfloat16)
            sum_copy(0, way, sub).start()

    def scatter_step(step, carry):
        make_terms(step + 2)
        for sub in range(PIECES):
            for way in range(2):
                sum_copy(step, way, sub).wait_recv()
                rows = slice(sub * piece, (sub + 1) * piece)
                total = sums[way, step + 1, rows, :].astype(jnp.float32) + terms[way, rows, :]
                sums[way, step + 1, rows, :] = total.astype(jnp.bfloat16)
                sum_copy(step + 1, way, sub).start()
        return carry

    lax.fori_loop(0, n_mp - 2, scatter_step, 0)
    make_terms(n_mp)
    for sub in range(PIECES):
        for way in range(2):
            sum_copy(n_mp - 2, way, sub).wait_recv()
            rows = slice(sub * piece, (sub + 1) * piece)
            total = sums[way, n_mp - 1, rows, :].astype(jnp.float32) + terms[way, rows, :]
            start = way * half + sub * piece
            out_ref[start:start + piece, :] = total.astype(jnp.bfloat16)

    def drain(step, carry):
        for sub in range(PIECES):
            for way in range(2):
                x_copy(step, way, sub).wait_send()
                sum_copy(step, way, sub).wait_send()
        return carry

    lax.fori_loop(0, n_mp - 1, drain, 0)
    for w in range(4):
        for i in range(2 * groups - 1):
            weight_copy(w, me_dp, shards[w], i, partner).wait_send()


def local(
    pair_tokens,
    norm_gain,
    q_weight,
    k_weight,
    value_weight,
    o_weight,
    pair_row,
    pair_span,
    block_ids,
):
    dp_count = lax.axis_size("dp")
    mp_count = lax.axis_size("mp")
    own_index = lax.axis_index("dp")
    pairs_dev = pair_tokens.shape[0]
    pair_cap = pair_tokens.shape[1]
    width_local = pair_tokens.shape[2]
    all_pairs = pair_row.shape[0]
    most_sent = -(-pairs_dev // dp_count)
    tok_dev = block_ids.shape[0]
    rows_dev = tok_dev // ROW_TOKENS
    owners_all = (pair_row // rows_dev).reshape(dp_count, pairs_dev)
    same_owner = owners_all[:, :, None] == owners_all[:, None, :]
    listed = jnp.arange(pairs_dev)
    before = listed[None, :] < listed[:, None]
    rank_all = jnp.sum((same_owner & before[None]).astype(jnp.int32), axis=2)
    own_owner = lax.dynamic_index_in_dim(owners_all, own_index, 0, keepdims=False)
    own_rank = lax.dynamic_index_in_dim(rank_all, own_index, 0, keepdims=False)
    slots = jnp.arange(pair_cap, dtype=jnp.int32)
    sent = dp_count * most_sent
    own_slot = ((own_owner * most_sent + own_rank)[:, None] * pair_cap + slots[None, :]).reshape(-1)
    pick = (jnp.arange(sent * pair_cap)[:, None] == own_slot[None, :]).astype(jnp.bfloat16)
    outgoing = jnp.dot(
        pick,
        pair_tokens.reshape(pairs_dev * pair_cap, width_local),
        preferred_element_type=jnp.float32,
    ).astype(jnp.bfloat16)
    incoming = lax.all_to_all(
        outgoing.reshape(dp_count, most_sent * pair_cap, width_local),
        "dp",
        split_axis=0,
        concat_axis=0,
        tiled=True,
    )
    length = pair_span[:, 1] - pair_span[:, 0]
    source = jnp.arange(all_pairs, dtype=jnp.int32) // pairs_dev
    first = (pair_row % rows_dev) * ROW_TOKENS + pair_span[:, 0]
    place = source * most_sent + rank_all.reshape(-1)
    mine = owners_all.reshape(-1) == own_index
    match = (jnp.arange(sent)[:, None] == place[None, :]) & mine[None, :]
    first_of = jnp.sum(jnp.where(match, first[None, :], 0), axis=1)
    length_of = jnp.sum(jnp.where(match, length[None, :], 0), axis=1)
    placement_map = jnp.where(
        slots[None, :] < length_of[:, None], first_of[:, None] + slots[None, :], tok_dev
    ).reshape(-1)
    put = (jnp.arange(tok_dev)[:, None] == placement_map[None, :]).astype(jnp.bfloat16)
    packed_local = jnp.dot(
        put,
        incoming.reshape(sent * pair_cap, width_local),
        preferred_element_type=jnp.float32,
    ).astype(jnp.bfloat16)

    ids_rows = block_ids.reshape(rows_dev, ROW_TOKENS)
    visible = jax.vmap(row_mask)(ids_rows)
    token_position = (jnp.sum(visible.astype(jnp.int32), axis=2) - 1).reshape(tok_dev)
    half = HEAD_SIZE // 2
    freq = 500000.0 ** (-(jnp.arange(half, dtype=jnp.float32) * 2.0 / HEAD_SIZE))
    angle = token_position.astype(jnp.float32)[:, None] * freq[None, :]
    cosine = jnp.cos(angle)
    sine = jnp.sin(angle)
    cosine = jnp.concatenate([cosine, cosine], axis=1)
    sine = jnp.concatenate([-sine, sine], axis=1)
    seen = visible.astype(jnp.int32).reshape(tok_dev, ROW_TOKENS)

    q_width = q_weight.shape[1]
    k_width = k_weight.shape[1]
    width = norm_gain.shape[0]
    far = dp_count - 1
    vmem = pl.BlockSpec(memory_space=pltpu.VMEM)
    anyspace = pl.BlockSpec(memory_space=pl.ANY)
    bf16 = jnp.bfloat16
    return pl.pallas_call(
        functools.partial(kernel, dp_count, mp_count),
        out_shape=jax.ShapeDtypeStruct((tok_dev, width_local), bf16),
        in_specs=[anyspace, vmem, anyspace, anyspace, anyspace, anyspace, vmem, vmem, vmem],
        out_specs=vmem,
        scratch_shapes=[
            pltpu.VMEM((mp_count, tok_dev, width_local), bf16),
            pltpu.VMEM((width, q_width), bf16),
            pltpu.VMEM((width, k_width), bf16),
            pltpu.VMEM((width, k_width), bf16),
            pltpu.VMEM((o_weight.shape[0], width), bf16),
            pltpu.VMEM((tok_dev, q_width + 2 * k_width), jnp.float32),
            pltpu.VMEM((tok_dev, q_width), bf16),
            pltpu.VMEM((2, mp_count, tok_dev // 2, width_local), bf16),
            pltpu.VMEM((2, tok_dev // 2, width_local), jnp.float32),
            pltpu.SemaphoreType.DMA((5,)),
            pltpu.SemaphoreType.DMA((4, far)),
            pltpu.SemaphoreType.DMA((4, dp_count)),
            pltpu.SemaphoreType.DMA((2, PIECES, mp_count - 1)),
            pltpu.SemaphoreType.DMA((2, PIECES, mp_count - 1)),
            pltpu.SemaphoreType.DMA((2, PIECES, mp_count - 1)),
            pltpu.SemaphoreType.DMA((2, PIECES, mp_count - 1)),
        ],
        compiler_params=pltpu.CompilerParams(
            collective_id=0, has_side_effects=True, vmem_limit_bytes=60 * 1024 * 1024
        ),
    )(
        packed_local,
        norm_gain.reshape(mp_count, width_local),
        q_weight,
        k_weight,
        value_weight,
        o_weight,
        cosine,
        sine,
        seen,
    )


def solution(mesh):
    placed = (
        P("dp", None, "mp"),
        P(),
        P("dp", "mp"),
        P("dp", "mp"),
        P("dp", "mp"),
        P("mp", "dp"),
        P(),
        P(),
        P("dp"),
    )
    return jax.shard_map(
        local, mesh=mesh, in_specs=placed, out_specs=P("dp", "mp"), check_vma=False
    )
```

```python
import functools

import jax
import jax.numpy as jnp
import numpy as np
from jax import lax
from jax.experimental import pallas as pl
from jax.experimental.pallas import tpu as pltpu
from jax.sharding import PartitionSpec as P

HEAD_SIZE = 128
ROW_TOKENS = 128
QUERY_PER_KV = 4
PIECES = 2
MESH = pl.DeviceIdType.MESH


def ring_member(place, count):
    place = lax.rem(place + 2 * count, count)
    return jnp.where(place < count // 2, 2 * place, 2 * (count - 1 - place) + 1)


def pieces_of_output(n_mp, width, chunk):
    if width != 2 * chunk:
        return 1
    order = list(range(0, n_mp, 2)) + list(range(1, n_mp, 2))[::-1]
    apart = all(order[p - 1] // 2 != order[(p + 1) % n_mp] // 2 for p in range(n_mp))
    return 2 if apart else 1


def kernel(
    n_dp, n_mp,
    map_ref, tok_ref, gain_ref, q_ref, k_ref, v_ref, o_ref, ids_ref, freq_ref,
    out_ref,
    xin, xg, wq, wk, wv, wo, acc, square, attn, sums, terms, cos_ref, sin_ref, vis_ref,
    own_sem, t_send, t_recv, w_send, w_recv, x_send, x_recv, s_send, s_recv,
):
    me_dp = lax.axis_index("dp")
    me_mp = lax.axis_index("mp")

    def place_of(g):
        return jnp.where(lax.rem(g, 2) == 0, g // 2, n_mp - 1 - g // 2)

    place = place_of(me_mp)
    sides = (ring_member(place + 1, n_mp), ring_member(place - 1, n_mp))
    groups = n_dp // 2
    core = lax.rem(me_dp, 2)
    partner = me_dp + 1 - 2 * core
    others = [lax.rem(me_dp + 2 * j, n_dp) for j in range(1, groups)]
    tokens, chunk = out_ref.shape
    half = tokens // 2
    piece = half // PIECES
    block = tok_ref.shape[0] // n_dp
    width = o_ref.shape[1]
    n_out = pieces_of_output(n_mp, width, chunk)

    barrier = pltpu.get_barrier_semaphore()
    for side in sides:
        pl.semaphore_signal(barrier, inc=1, device_id={"mp": side}, device_id_type=MESH)
    for j in range(1, n_dp):
        peer = lax.rem(me_dp + j, n_dp)
        pl.semaphore_signal(barrier, inc=1, device_id={"dp": peer}, device_id_type=MESH)
    pl.semaphore_wait(barrier, 2 + n_dp - 1)

    def token_rows(owner):
        return pl.ds(pl.multiple_of(owner * block, 16), block)

    def token_copy(j):
        peer = lax.rem(me_dp + j, n_dp)
        return pltpu.make_async_remote_copy(
            src_ref=tok_ref.at[token_rows(peer), :],
            dst_ref=xin.at[token_rows(me_dp), :],
            send_sem=t_send.at[j - 1],
            recv_sem=t_recv.at[me_dp],
            device_id={"dp": peer},
            device_id_type=MESH,
        )

    def token_arrival(j):
        peer = lax.rem(me_dp + j, n_dp)
        return pltpu.make_async_remote_copy(
            src_ref=tok_ref.at[token_rows(peer), :],
            dst_ref=xin.at[token_rows(peer), :],
            send_sem=t_send.at[j - 1],
            recv_sem=t_recv.at[peer],
            device_id={"dp": peer},
            device_id_type=MESH,
        )

    own_tokens = pltpu.make_async_copy(
        tok_ref.at[token_rows(me_dp), :], xin.at[token_rows(me_dp), :], own_sem.at[4]
    )
    for j in range(1, n_dp):
        token_copy(j).start()
    own_tokens.start()

    def hop_of(g):
        gap = lax.rem(place_of(g) - place + n_mp, n_mp)
        gap = jnp.where(gap == 0, n_mp, gap)
        return jnp.minimum(gap, jnp.where(gap == n_mp, n_mp, n_mp - gap))

    def out_columns(which, owner):
        if n_out == 1:
            return owner * 0
        later = (hop_of(2 * owner + 1) < hop_of(2 * owner)).astype(jnp.int32)
        return chunk * (later if which == 3 else 1 - later)

    def part(which, owner):
        if which >= 3:
            start = owner * width + out_columns(which, owner)
            return wo.at[:, pl.ds(pl.multiple_of(start, 128), width // n_out)]
        full = (wq, wk, wv)[which]
        depth = q_ref.shape[0]
        return full.at[pl.ds(pl.multiple_of(owner * depth, 16), depth), :]

    def shard(which):
        if which >= 3:
            start = out_columns(which, me_dp)
            return o_ref.at[:, pl.ds(pl.multiple_of(start, 128), width // n_out)]
        return (q_ref, k_ref, v_ref)[which]

    kinds = 3 + n_out

    def weight_copy(which, owner, source, slot, peer):
        return pltpu.make_async_remote_copy(
            src_ref=source,
            dst_ref=part(which, owner),
            send_sem=w_send.at[which, slot],
            recv_sem=w_recv.at[which, owner],
            device_id={"dp": peer},
            device_id_type=MESH,
        )

    def x_copy(step, way, sub):
        sign = -1 if way == 0 else 1
        chunk_of = ring_member(place + sign * step, n_mp)
        rows = pl.ds(way * half + sub * piece, piece)
        ref = xg.at[chunk_of, rows, :]
        return pltpu.make_async_remote_copy(
            src_ref=ref,
            dst_ref=ref,
            send_sem=x_send.at[way, sub, step],
            recv_sem=x_recv.at[way, sub, step],
            device_id={"mp": sides[way]},
            device_id_type=MESH,
        )

    def x_arrival(step, way, sub):
        sign = -1 if way == 0 else 1
        chunk_of = ring_member(place + sign * (step + 1), n_mp)
        rows = pl.ds(way * half + sub * piece, piece)
        ref = xg.at[chunk_of, rows, :]
        return pltpu.make_async_remote_copy(
            src_ref=ref,
            dst_ref=ref,
            send_sem=x_send.at[way, sub, step],
            recv_sem=x_recv.at[way, sub, step],
            device_id={"mp": sides[way]},
            device_id_type=MESH,
        )

    owns = [
        pltpu.make_async_copy(
            (q_ref, k_ref, v_ref)[w],
            part(w, me_dp),
            own_sem.at[w],
        )
        for w in range(3)
    ]
    owns.append(
        pltpu.make_async_copy(
            o_ref,
            wo.at[:, pl.ds(pl.multiple_of(me_dp * width, 128), width)],
            own_sem.at[3],
        )
    )
    for w in range(kinds):
        for j, peer in enumerate(others):
            weight_copy(w, me_dp, shard(w), 1 + j, peer).start()
    for w in range(3):
        owns[w].start()
        weight_copy(w, me_dp, shard(w), 0, partner).start()

    def tables(r, carry):
        rows = pl.ds(pl.multiple_of(r * ROW_TOKENS, ROW_TOKENS), ROW_TOKENS)
        ids_j = jnp.broadcast_to(ids_ref[pl.ds(r, 1), :], (ROW_TOKENS, ROW_TOKENS)).astype(
            jnp.float32
        )
        ids_i = jnp.transpose(ids_j)
        pair_i = jnp.floor((ids_i + 0.5) * (1.0 / 3.0))
        pair_j = jnp.floor((ids_j + 0.5) * (1.0 / 3.0))
        at_i = lax.broadcasted_iota(jnp.int32, (ROW_TOKENS, ROW_TOKENS), 0)
        at_j = lax.broadcasted_iota(jnp.int32, (ROW_TOKENS, ROW_TOKENS), 1)
        hidden = (ids_i - 3.0 * pair_i == 2.0) & (ids_j - 3.0 * pair_j == 1.0)
        seen = jnp.where((at_j <= at_i) & (pair_i == pair_j), 1.0, 0.0)
        seen = jnp.where(hidden, 0.0, seen)
        vis_ref[rows, :] = seen
        angle = (jnp.sum(seen, axis=1, keepdims=True) - 1.0) * freq_ref[...]
        lane = lax.broadcasted_iota(jnp.int32, (ROW_TOKENS, HEAD_SIZE), 1)
        sine = jnp.sin(angle)
        cos_ref[rows, :] = jnp.cos(angle)
        sin_ref[rows, :] = jnp.where(lane < HEAD_SIZE // 2, -sine, sine)
        return carry

    lax.fori_loop(0, tokens // ROW_TOKENS, tables, 0)
    acc[...] = jnp.zeros_like(acc)
    square[...] = jnp.zeros_like(square)

    own_tokens.wait()
    for j in range(1, n_dp):
        token_arrival(j).wait_recv()
    for sub in range(PIECES):
        for way in range(2):
            start = way * half + sub * piece
            at = lax.broadcasted_iota(jnp.int32, (piece, n_dp * block), 0) + start
            put = jnp.where(at == map_ref[...], 1.0, 0.0).astype(jnp.bfloat16)
            xg[me_mp, start:start + piece, :] = jnp.dot(
                put, xin[...], preferred_element_type=jnp.float32
            ).astype(jnp.bfloat16)
            x_copy(0, way, sub).start()
    owns[3].start()
    for w in range(3, kinds):
        weight_copy(w, me_dp, shard(w), 0, partner).start()

    def pass_weight(w):
        for j in range(1, groups):
            owner = lax.rem(me_dp + n_dp - 2 * j, n_dp)
            weight_copy(w, owner, part(w, owner), 0, partner).wait_recv()
            weight_copy(w, owner, part(w, owner), groups + j - 1, partner).start()

    def weight_done(w):
        for i in range(groups):
            owner = lax.rem(partner + 2 * i, n_dp)
            weight_copy(w, owner, part(w, owner), 0, partner).wait_recv()

    q_width = wq.shape[1]
    k_width = wk.shape[1]

    def project(way, g):
        halves = pl.ds(pl.multiple_of(way * half, 16), half)
        wide = xg[g, halves, :].astype(jnp.float32)
        square[halves, :] += jnp.sum(wide * wide, axis=1, keepdims=True)
        columns = pl.ds(pl.multiple_of(g * chunk, 128), chunk)
        scaled = (wide * gain_ref[:, columns]).astype(jnp.bfloat16)
        rows = pl.ds(pl.multiple_of(g * chunk, 16), chunk)
        acc[halves, 0:q_width] += jnp.dot(
            scaled, wq[rows, :], preferred_element_type=jnp.float32
        )
        acc[halves, q_width:q_width + k_width] += jnp.dot(
            scaled, wk[rows, :], preferred_element_type=jnp.float32
        )
        acc[halves, q_width + k_width:] += jnp.dot(
            scaled, wv[rows, :], preferred_element_type=jnp.float32
        )

    def project_step(hop, near):
        def one(way, carry):
            g = ring_member(place + jnp.where(way == 0, -hop, hop), n_mp)
            is_near = (g * chunk) // (2 * q_ref.shape[0]) == me_dp // 2

            @pl.when(is_near == near)
            def _():
                project(way, g)

            return carry

        lax.fori_loop(0, 2, one, 0)

    for w in range(3):
        owns[w].wait()
        owner = partner
        weight_copy(w, owner, part(w, owner), 0, partner).wait_recv()

    def gather_step(step, carry):
        project_step(step, True)
        for sub in range(PIECES):
            for way in range(2):
                x_arrival(step, way, sub).wait_recv()
                x_copy(step + 1, way, sub).start()
        return carry

    def weight_rest(w):
        for i in range(1, groups):
            owner = lax.rem(partner + 2 * i, n_dp)
            weight_copy(w, owner, part(w, owner), 0, partner).wait_recv()

    late = max(n_mp - 3, 0)
    lax.fori_loop(0, late, gather_step, 0)
    pass_weight(0)
    lax.fori_loop(late, n_mp - 2, gather_step, 0)
    pass_weight(1)
    pass_weight(2)
    project_step(n_mp - 2, True)
    for w in range(3):
        weight_rest(w)

    def project_far(hop, carry):
        project_step(hop, False)
        return carry

    lax.fori_loop(0, n_mp - 1, project_far, 0)
    for sub in range(PIECES):
        for way in range(2):
            x_arrival(n_mp - 2, way, sub).wait_recv()

    def project_last(way, carry):
        project(way, ring_member(place + jnp.where(way == 0, 1 - n_mp, n_mp - 1), n_mp))
        return carry

    lax.fori_loop(0, 2, project_last, 0)
    acc[...] = acc[...] * lax.rsqrt(square[...] / (n_mp * chunk) + 1e-05)

    def turn(u, cosine, sine):
        return (u * cosine + pltpu.roll(u, HEAD_SIZE // 2, 1) * sine).astype(jnp.bfloat16)

    def attend(r, carry):
        rows = pl.ds(pl.multiple_of(r * ROW_TOKENS, ROW_TOKENS), ROW_TOKENS)
        cosine = cos_ref[rows, :]
        sine = sin_ref[rows, :]
        seen = vis_ref[rows, :] > 0.5
        for kv in range(k_width // HEAD_SIZE):
            at_k = q_width + kv * HEAD_SIZE
            key = turn(acc[rows, at_k:at_k + HEAD_SIZE], cosine, sine)
            value = acc[rows, at_k + k_width:at_k + k_width + HEAD_SIZE].astype(jnp.bfloat16)
            for h in range(kv * QUERY_PER_KV, (kv + 1) * QUERY_PER_KV):
                at = slice(h * HEAD_SIZE, (h + 1) * HEAD_SIZE)
                query = turn(acc[rows, at], cosine, sine)
                scores = lax.dot_general(
                    query, key, (((1,), (1,)), ((), ())), preferred_element_type=jnp.float32
                ) * HEAD_SIZE ** (-0.5)
                scores = jnp.where(seen, scores, -1e30)
                expo = jnp.exp(scores - jnp.max(scores, axis=-1, keepdims=True))
                probs = (expo / jnp.sum(expo, axis=-1, keepdims=True)).astype(jnp.bfloat16)
                attn[rows, at] = jnp.dot(
                    probs, value, preferred_element_type=jnp.float32
                ).astype(jnp.bfloat16)
        return carry

    lax.fori_loop(0, tokens // ROW_TOKENS, attend, 0)
    owns[3].wait()
    pass_weight(3)
    weight_done(3)

    def make_terms(hop):
        for way in range(2):
            sign = -1 if way == 0 else 1
            g = ring_member(place + sign * hop, n_mp)
            columns = pl.ds(pl.multiple_of(g * chunk, 128), chunk)
            terms[way] = jnp.dot(
                attn[way * half:(way + 1) * half, :],
                wo[:, columns],
                preferred_element_type=jnp.float32,
            )

    def sum_copy(slot, way, sub):
        rows = pl.ds(sub * piece, piece)
        return pltpu.make_async_remote_copy(
            src_ref=sums.at[way, slot, rows, :],
            dst_ref=sums.at[way, slot + 1, rows, :],
            send_sem=s_send.at[way, sub, slot],
            recv_sem=s_recv.at[way, sub, slot],
            device_id={"mp": sides[way]},
            device_id_type=MESH,
        )

    make_terms(1)
    for sub in range(PIECES):
        for way in range(2):
            rows = slice(sub * piece, (sub + 1) * piece)
            sums[way, 0, rows, :] = terms[way, rows, :].astype(jnp.bfloat16)
            sum_copy(0, way, sub).start()

    for w in range(4, kinds):
        pass_weight(w)
        weight_done(w)

    def scatter_step(step, carry):
        make_terms(step + 2)
        for sub in range(PIECES):
            for way in range(2):
                sum_copy(step, way, sub).wait_recv()
                rows = slice(sub * piece, (sub + 1) * piece)
                total = sums[way, step + 1, rows, :].astype(jnp.float32) + terms[way, rows, :]
                sums[way, step + 1, rows, :] = total.astype(jnp.bfloat16)
                sum_copy(step + 1, way, sub).start()
        return carry

    lax.fori_loop(0, n_mp - 2, scatter_step, 0)
    make_terms(n_mp)
    for sub in range(PIECES):
        for way in range(2):
            sum_copy(n_mp - 2, way, sub).wait_recv()
            rows = slice(sub * piece, (sub + 1) * piece)
            total = sums[way, n_mp - 1, rows, :].astype(jnp.float32) + terms[way, rows, :]
            start = way * half + sub * piece
            out_ref[start:start + piece, :] = total.astype(jnp.bfloat16)

    def drain(step, carry):
        for sub in range(PIECES):
            for way in range(2):
                x_copy(step, way, sub).wait_send()
                sum_copy(step, way, sub).wait_send()
        return carry

    lax.fori_loop(0, n_mp - 1, drain, 0)
    for j in range(1, n_dp):
        token_copy(j).wait_send()
    for w in range(kinds):
        for i in range(2 * groups - 1):
            weight_copy(w, me_dp, shard(w), i, partner).wait_send()


def local(
    pair_tokens,
    norm_gain,
    q_weight,
    k_weight,
    value_weight,
    o_weight,
    pair_row,
    pair_span,
    block_ids,
):
    dp_count = lax.axis_size("dp")
    mp_count = lax.axis_size("mp")
    own_index = lax.axis_index("dp")
    pairs_dev = pair_tokens.shape[0]
    pair_cap = pair_tokens.shape[1]
    width_local = pair_tokens.shape[2]
    all_pairs = pair_row.shape[0]
    most_sent = -(-pairs_dev // dp_count)
    tok_dev = block_ids.shape[0]
    rows_dev = tok_dev // ROW_TOKENS
    owners_all = (pair_row // rows_dev).reshape(dp_count, pairs_dev)
    same_owner = owners_all[:, :, None] == owners_all[:, None, :]
    listed = jnp.arange(pairs_dev)
    before = listed[None, :] < listed[:, None]
    rank_all = jnp.sum((same_owner & before[None]).astype(jnp.int32), axis=2)
    own_owner = lax.dynamic_index_in_dim(owners_all, own_index, 0, keepdims=False)
    own_rank = lax.dynamic_index_in_dim(rank_all, own_index, 0, keepdims=False)
    slots = jnp.arange(pair_cap, dtype=jnp.int32)
    sent = dp_count * most_sent
    own_slot = ((own_owner * most_sent + own_rank)[:, None] * pair_cap + slots[None, :]).reshape(-1)
    pick = (jnp.arange(sent * pair_cap)[:, None] == own_slot[None, :]).astype(jnp.bfloat16)
    outgoing = jnp.dot(
        pick,
        pair_tokens.reshape(pairs_dev * pair_cap, width_local),
        preferred_element_type=jnp.float32,
    ).astype(jnp.bfloat16)
    length = pair_span[:, 1] - pair_span[:, 0]
    source = jnp.arange(all_pairs, dtype=jnp.int32) // pairs_dev
    first = (pair_row % rows_dev) * ROW_TOKENS + pair_span[:, 0]
    place = source * most_sent + rank_all.reshape(-1)
    mine = owners_all.reshape(-1) == own_index
    match = (jnp.arange(sent)[:, None] == place[None, :]) & mine[None, :]
    first_of = jnp.sum(jnp.where(match, first[None, :], 0), axis=1)
    length_of = jnp.sum(jnp.where(match, length[None, :], 0), axis=1)
    placement_map = jnp.where(
        slots[None, :] < length_of[:, None], first_of[:, None] + slots[None, :], tok_dev
    ).reshape(-1)
    half = HEAD_SIZE // 2
    freq = 500000.0 ** (-(np.arange(half, dtype=np.float32) * 2.0 / HEAD_SIZE))
    freq = np.concatenate([freq, freq])[None, :].astype(np.float32)

    q_width = q_weight.shape[1]
    k_width = k_weight.shape[1]
    width = norm_gain.shape[0]
    far = dp_count - 1
    vmem = pl.BlockSpec(memory_space=pltpu.VMEM)
    anyspace = pl.BlockSpec(memory_space=pl.ANY)
    bf16 = jnp.bfloat16
    return pl.pallas_call(
        functools.partial(kernel, dp_count, mp_count),
        out_shape=jax.ShapeDtypeStruct((tok_dev, width_local), bf16),
        in_specs=[vmem, anyspace, vmem, anyspace, anyspace, anyspace, anyspace, vmem, vmem],
        out_specs=vmem,
        scratch_shapes=[
            pltpu.VMEM((sent * pair_cap, width_local), bf16),
            pltpu.VMEM((mp_count, tok_dev, width_local), bf16),
            pltpu.VMEM((width, q_width), bf16),
            pltpu.VMEM((width, k_width), bf16),
            pltpu.VMEM((width, k_width), bf16),
            pltpu.VMEM((o_weight.shape[0], width), bf16),
            pltpu.VMEM((tok_dev, q_width + 2 * k_width), jnp.float32),
            pltpu.VMEM((tok_dev, 1), jnp.float32),
            pltpu.VMEM((tok_dev, q_width), bf16),
            pltpu.VMEM((2, mp_count, tok_dev // 2, width_local), bf16),
            pltpu.VMEM((2, tok_dev // 2, width_local), jnp.float32),
            pltpu.VMEM((tok_dev, HEAD_SIZE), jnp.float32),
            pltpu.VMEM((tok_dev, HEAD_SIZE), jnp.float32),
            pltpu.VMEM((tok_dev, ROW_TOKENS), jnp.float32),
            pltpu.SemaphoreType.DMA((5,)),
            pltpu.SemaphoreType.DMA((far,)),
            pltpu.SemaphoreType.DMA((dp_count,)),
            pltpu.SemaphoreType.DMA((5, far)),
            pltpu.SemaphoreType.DMA((5, dp_count)),
            pltpu.SemaphoreType.DMA((2, PIECES, mp_count - 1)),
            pltpu.SemaphoreType.DMA((2, PIECES, mp_count - 1)),
            pltpu.SemaphoreType.DMA((2, PIECES, mp_count - 1)),
            pltpu.SemaphoreType.DMA((2, PIECES, mp_count - 1)),
        ],
        compiler_params=pltpu.CompilerParams(
            collective_id=0, has_side_effects=True, vmem_limit_bytes=60 * 1024 * 1024
        ),
    )(
        placement_map[None, :],
        outgoing,
        norm_gain[None, :],
        q_weight,
        k_weight,
        value_weight,
        o_weight,
        block_ids.reshape(rows_dev, ROW_TOKENS),
        jnp.asarray(freq),
    )


def solution(mesh):
    placed = (
        P("dp", None, "mp"),
        P(),
        P("dp", "mp"),
        P("dp", "mp"),
        P("dp", "mp"),
        P("mp", "dp"),
        P(),
        P(),
        P("dp"),
    )
    return jax.shard_map(
        local, mesh=mesh, in_specs=placed, out_specs=P("dp", "mp"), check_vma=False
    )
```

```python
import functools

import jax
import jax.numpy as jnp
import numpy as np
from jax import lax
from jax.experimental import pallas as pl
from jax.experimental.pallas import tpu as pltpu
from jax.sharding import PartitionSpec as P

HEAD_SIZE = 128
ROW_TOKENS = 128
QUERY_PER_KV = 4
PIECES = 2
SLICES = 4
MESH = pl.DeviceIdType.MESH


def ring_member(place, count):
    place = lax.rem(place + 2 * count, count)
    return jnp.where(place < count // 2, 2 * place, 2 * (count - 1 - place) + 1)


def pieces_of_output(n_mp, width, chunk):
    if width != 2 * chunk:
        return 1
    order = list(range(0, n_mp, 2)) + list(range(1, n_mp, 2))[::-1]
    apart = all(order[p - 1] // 2 != order[(p + 1) % n_mp] // 2 for p in range(n_mp))
    return 2 if apart else 1


def kernel(
    n_dp, n_mp,
    map_ref, tok_ref, gain_ref, q_ref, k_ref, v_ref, o_ref, ids_ref, freq_ref,
    out_ref,
    xin, xg, wq, wk, wv, wo, acc, square, attn, sums, terms, cos_ref, sin_ref, vis_ref, put_ref,
    own_sem, t_send, t_recv, w_send, w_recv, x_send, x_recv, s_send, s_recv,
):
    me_dp = lax.axis_index("dp")
    me_mp = lax.axis_index("mp")

    def place_of(g):
        return jnp.where(lax.rem(g, 2) == 0, g // 2, n_mp - 1 - g // 2)

    place = place_of(me_mp)
    sides = (ring_member(place + 1, n_mp), ring_member(place - 1, n_mp))
    groups = n_dp // 2
    core = lax.rem(me_dp, 2)
    partner = me_dp + 1 - 2 * core
    others = [lax.rem(me_dp + 2 * j, n_dp) for j in range(1, groups)]
    tokens, chunk = out_ref.shape
    half = tokens // 2
    piece = half // PIECES
    block = tok_ref.shape[0] // n_dp
    width = o_ref.shape[1]
    n_out = pieces_of_output(n_mp, width, chunk)

    barrier = pltpu.get_barrier_semaphore()
    for side in sides:
        pl.semaphore_signal(barrier, inc=1, device_id={"mp": side}, device_id_type=MESH)
    for j in range(1, n_dp):
        peer = lax.rem(me_dp + j, n_dp)
        pl.semaphore_signal(barrier, inc=1, device_id={"dp": peer}, device_id_type=MESH)
    pl.semaphore_wait(barrier, 2 + n_dp - 1)

    def token_rows(owner):
        return pl.ds(pl.multiple_of(owner * block, 16), block)

    slice_width = chunk // SLICES

    def token_slice(sub):
        return pl.ds(sub * slice_width, slice_width)

    def token_copy(j, sub):
        peer = lax.rem(me_dp + j, n_dp)
        return pltpu.make_async_remote_copy(
            src_ref=tok_ref.at[token_rows(peer), token_slice(sub)],
            dst_ref=xin.at[token_rows(me_dp), token_slice(sub)],
            send_sem=t_send.at[sub, j - 1],
            recv_sem=t_recv.at[sub, me_dp],
            device_id={"dp": peer},
            device_id_type=MESH,
        )

    def token_arrival(j, sub):
        peer = lax.rem(me_dp + j, n_dp)
        return pltpu.make_async_remote_copy(
            src_ref=tok_ref.at[token_rows(peer), token_slice(sub)],
            dst_ref=xin.at[token_rows(peer), token_slice(sub)],
            send_sem=t_send.at[sub, j - 1],
            recv_sem=t_recv.at[sub, peer],
            device_id={"dp": peer},
            device_id_type=MESH,
        )

    own_tokens = pltpu.make_async_copy(
        tok_ref.at[token_rows(me_dp), :], xin.at[token_rows(me_dp), :], own_sem.at[4]
    )
    for sub in range(SLICES):
        for j in range(1, n_dp):
            token_copy(j, sub).start()
    own_tokens.start()

    def hop_of(g):
        gap = lax.rem(place_of(g) - place + n_mp, n_mp)
        gap = jnp.where(gap == 0, n_mp, gap)
        return jnp.minimum(gap, jnp.where(gap == n_mp, n_mp, n_mp - gap))

    def out_columns(which, owner):
        if n_out == 1:
            return owner * 0
        later = (hop_of(2 * owner + 1) < hop_of(2 * owner)).astype(jnp.int32)
        return chunk * (later if which == 3 else 1 - later)

    def part(which, owner):
        if which >= 3:
            start = owner * width + out_columns(which, owner)
            return wo.at[:, pl.ds(pl.multiple_of(start, 128), width // n_out)]
        full = (wq, wk, wv)[which]
        depth = q_ref.shape[0]
        return full.at[pl.ds(pl.multiple_of(owner * depth, 16), depth), :]

    def shard(which):
        if which >= 3:
            start = out_columns(which, me_dp)
            return o_ref.at[:, pl.ds(pl.multiple_of(start, 128), width // n_out)]
        return (q_ref, k_ref, v_ref)[which]

    kinds = 3 + n_out

    def weight_copy(which, owner, source, slot, peer):
        return pltpu.make_async_remote_copy(
            src_ref=source,
            dst_ref=part(which, owner),
            send_sem=w_send.at[which, slot],
            recv_sem=w_recv.at[which, owner],
            device_id={"dp": peer},
            device_id_type=MESH,
        )

    def x_copy(step, way, sub):
        sign = -1 if way == 0 else 1
        chunk_of = ring_member(place + sign * step, n_mp)
        ref = xg.at[chunk_of, pl.ds(way * half, half), token_slice(sub)]
        return pltpu.make_async_remote_copy(
            src_ref=ref,
            dst_ref=ref,
            send_sem=x_send.at[way, sub, step],
            recv_sem=x_recv.at[way, sub, step],
            device_id={"mp": sides[way]},
            device_id_type=MESH,
        )

    def x_arrival(step, way, sub):
        sign = -1 if way == 0 else 1
        chunk_of = ring_member(place + sign * (step + 1), n_mp)
        ref = xg.at[chunk_of, pl.ds(way * half, half), token_slice(sub)]
        return pltpu.make_async_remote_copy(
            src_ref=ref,
            dst_ref=ref,
            send_sem=x_send.at[way, sub, step],
            recv_sem=x_recv.at[way, sub, step],
            device_id={"mp": sides[way]},
            device_id_type=MESH,
        )

    owns = [
        pltpu.make_async_copy(
            (q_ref, k_ref, v_ref)[w],
            part(w, me_dp),
            own_sem.at[w],
        )
        for w in range(3)
    ]
    owns.append(
        pltpu.make_async_copy(
            o_ref,
            wo.at[:, pl.ds(pl.multiple_of(me_dp * width, 128), width)],
            own_sem.at[3],
        )
    )
    def second_chunk(owner):
        return (owner * width + out_columns(4, owner)) // chunk

    def second_stage(owner):
        hop = hop_of(second_chunk(owner))
        return jnp.where(hop == n_mp, 2, jnp.where(hop > 2, 1, 0))

    held = second_stage(me_dp) == 2

    def send_second():
        for j, peer in enumerate(others):
            weight_copy(4, me_dp, shard(4), 1 + j, peer).start()

    for w in range(min(kinds, 4)):
        for j, peer in enumerate(others):
            weight_copy(w, me_dp, shard(w), 1 + j, peer).start()
    if kinds == 5:
        pl.when(jnp.logical_not(held))(send_second)
    for w in range(3):
        owns[w].start()
        weight_copy(w, me_dp, shard(w), 0, partner).start()

    def tables(r, carry):
        rows = pl.ds(pl.multiple_of(r * ROW_TOKENS, ROW_TOKENS), ROW_TOKENS)
        ids_j = jnp.broadcast_to(ids_ref[pl.ds(r, 1), :], (ROW_TOKENS, ROW_TOKENS)).astype(
            jnp.float32
        )
        ids_i = jnp.transpose(ids_j)
        pair_i = jnp.floor((ids_i + 0.5) * (1.0 / 3.0))
        pair_j = jnp.floor((ids_j + 0.5) * (1.0 / 3.0))
        at_i = lax.broadcasted_iota(jnp.int32, (ROW_TOKENS, ROW_TOKENS), 0)
        at_j = lax.broadcasted_iota(jnp.int32, (ROW_TOKENS, ROW_TOKENS), 1)
        hidden = (ids_i - 3.0 * pair_i == 2.0) & (ids_j - 3.0 * pair_j == 1.0)
        seen = jnp.where((at_j <= at_i) & (pair_i == pair_j), 1.0, 0.0)
        seen = jnp.where(hidden, 0.0, seen)
        vis_ref[rows, :] = seen
        angle = (jnp.sum(seen, axis=1, keepdims=True) - 1.0) * freq_ref[...]
        lane = lax.broadcasted_iota(jnp.int32, (ROW_TOKENS, HEAD_SIZE), 1)
        sine = jnp.sin(angle)
        cos_ref[rows, :] = jnp.cos(angle)
        sin_ref[rows, :] = jnp.where(lane < HEAD_SIZE // 2, -sine, sine)
        return carry

    lax.fori_loop(0, tokens // ROW_TOKENS, tables, 0)
    acc[...] = jnp.zeros_like(acc)
    square[...] = jnp.zeros_like(square)

    own_tokens.wait()
    at = lax.broadcasted_iota(jnp.int32, (tokens, n_dp * block), 0)
    put_ref[...] = jnp.where(at == map_ref[...], 1.0, 0.0).astype(jnp.bfloat16)
    for sub in range(SLICES):
        for j in range(1, n_dp):
            token_arrival(j, sub).wait_recv()
        columns = slice(sub * slice_width, (sub + 1) * slice_width)
        xg[me_mp, :, columns] = jnp.dot(
            put_ref[...], xin[:, columns], preferred_element_type=jnp.float32
        ).astype(jnp.bfloat16)
        for way in range(2):
            x_copy(0, way, sub).start()
    owns[3].start()
    for w in range(3, kinds):
        weight_copy(w, me_dp, shard(w), 0, partner).start()

    def pass_weight(w):
        for j in range(1, groups):
            owner = lax.rem(me_dp + n_dp - 2 * j, n_dp)
            weight_copy(w, owner, part(w, owner), 0, partner).wait_recv()
            weight_copy(w, owner, part(w, owner), groups + j - 1, partner).start()

    def weight_done(w):
        for i in range(groups):
            owner = lax.rem(partner + 2 * i, n_dp)
            weight_copy(w, owner, part(w, owner), 0, partner).wait_recv()

    q_width = wq.shape[1]
    k_width = wk.shape[1]

    def project(way, g):
        halves = pl.ds(pl.multiple_of(way * half, 16), half)
        wide = xg[g, halves, :].astype(jnp.float32)
        square[halves, :] += jnp.sum(wide * wide, axis=1, keepdims=True)
        columns = pl.ds(pl.multiple_of(g * chunk, 128), chunk)
        scaled = (wide * gain_ref[:, columns]).astype(jnp.bfloat16)
        rows = pl.ds(pl.multiple_of(g * chunk, 16), chunk)
        acc[halves, 0:q_width] += jnp.dot(
            scaled, wq[rows, :], preferred_element_type=jnp.float32
        )
        acc[halves, q_width:q_width + k_width] += jnp.dot(
            scaled, wk[rows, :], preferred_element_type=jnp.float32
        )
        acc[halves, q_width + k_width:] += jnp.dot(
            scaled, wv[rows, :], preferred_element_type=jnp.float32
        )

    def project_step(hop, near):
        def one(way, carry):
            g = ring_member(place + jnp.where(way == 0, -hop, hop), n_mp)
            is_near = (g * chunk) // (2 * q_ref.shape[0]) == me_dp // 2

            @pl.when(is_near == near)
            def _():
                project(way, g)

            return carry

        lax.fori_loop(0, 2, one, 0)

    for w in range(3):
        owns[w].wait()
        owner = partner
        weight_copy(w, owner, part(w, owner), 0, partner).wait_recv()

    def gather_step(step, carry):
        project_step(step, True)
        for sub in range(SLICES):
            for way in range(2):
                x_arrival(step, way, sub).wait_recv()
                x_copy(step + 1, way, sub).start()
        return carry

    def weight_rest(w):
        for i in range(1, groups):
            owner = lax.rem(partner + 2 * i, n_dp)
            weight_copy(w, owner, part(w, owner), 0, partner).wait_recv()

    late = max(n_mp - 3, 0)
    lax.fori_loop(0, late, gather_step, 0)
    pass_weight(0)
    lax.fori_loop(late, n_mp - 2, gather_step, 0)
    pass_weight(1)
    pass_weight(2)
    project_step(n_mp - 2, True)
    for w in range(3):
        weight_rest(w)

    def project_far(hop, carry):
        project_step(hop, False)
        return carry

    lax.fori_loop(0, n_mp - 1, project_far, 0)
    for sub in range(SLICES):
        for way in range(2):
            x_arrival(n_mp - 2, way, sub).wait_recv()

    def project_last(way, carry):
        project(way, ring_member(place + jnp.where(way == 0, 1 - n_mp, n_mp - 1), n_mp))
        return carry

    lax.fori_loop(0, 2, project_last, 0)
    acc[...] = acc[...] * lax.rsqrt(square[...] / (n_mp * chunk) + 1e-05)

    def turn(u, cosine, sine):
        return (u * cosine + pltpu.roll(u, HEAD_SIZE // 2, 1) * sine).astype(jnp.bfloat16)

    def attend(r, carry):
        rows = pl.ds(pl.multiple_of(r * ROW_TOKENS, ROW_TOKENS), ROW_TOKENS)
        cosine = cos_ref[rows, :]
        sine = sin_ref[rows, :]
        seen = vis_ref[rows, :] > 0.5
        for kv in range(k_width // HEAD_SIZE):
            at_k = q_width + kv * HEAD_SIZE
            key = turn(acc[rows, at_k:at_k + HEAD_SIZE], cosine, sine)
            value = acc[rows, at_k + k_width:at_k + k_width + HEAD_SIZE].astype(jnp.bfloat16)
            for h in range(kv * QUERY_PER_KV, (kv + 1) * QUERY_PER_KV):
                at = slice(h * HEAD_SIZE, (h + 1) * HEAD_SIZE)
                query = turn(acc[rows, at], cosine, sine)
                scores = lax.dot_general(
                    query, key, (((1,), (1,)), ((), ())), preferred_element_type=jnp.float32
                ) * HEAD_SIZE ** (-0.5)
                scores = jnp.where(seen, scores, -1e30)
                expo = jnp.exp(scores - jnp.max(scores, axis=-1, keepdims=True))
                probs = (expo / jnp.sum(expo, axis=-1, keepdims=True)).astype(jnp.bfloat16)
                attn[rows, at] = jnp.dot(
                    probs, value, preferred_element_type=jnp.float32
                ).astype(jnp.bfloat16)
        return carry

    lax.fori_loop(0, tokens // ROW_TOKENS, attend, 0)
    if kinds == 5:
        pl.when(held)(send_second)
    owns[3].wait()
    pass_weight(3)
    weight_done(3)

    def make_terms(hop):
        for way in range(2):
            sign = -1 if way == 0 else 1
            g = ring_member(place + sign * hop, n_mp)
            columns = pl.ds(pl.multiple_of(g * chunk, 128), chunk)
            terms[way] = jnp.dot(
                attn[way * half:(way + 1) * half, :],
                wo[:, columns],
                preferred_element_type=jnp.float32,
            )

    def sum_copy(slot, way, sub):
        rows = pl.ds(sub * piece, piece)
        return pltpu.make_async_remote_copy(
            src_ref=sums.at[way, slot, rows, :],
            dst_ref=sums.at[way, slot + 1, rows, :],
            send_sem=s_send.at[way, sub, slot],
            recv_sem=s_recv.at[way, sub, slot],
            device_id={"mp": sides[way]},
            device_id_type=MESH,
        )

    make_terms(1)
    for sub in range(PIECES):
        for way in range(2):
            rows = slice(sub * piece, (sub + 1) * piece)
            sums[way, 0, rows, :] = terms[way, rows, :].astype(jnp.bfloat16)
            sum_copy(0, way, sub).start()

    def second_pieces(stage):
        if kinds < 5:
            return
        for j in range(1, groups):
            owner = lax.rem(me_dp + n_dp - 2 * j, n_dp)

            @pl.when(second_stage(owner) == stage)
            def _():
                weight_copy(4, owner, part(4, owner), 0, partner).wait_recv()
                weight_copy(4, owner, part(4, owner), groups + j - 1, partner).start()

        for i in range(groups):
            owner = lax.rem(partner + 2 * i, n_dp)

            @pl.when(second_stage(owner) == stage)
            def _():
                weight_copy(4, owner, part(4, owner), 0, partner).wait_recv()

    second_pieces(0)

    def scatter_step(step, carry):
        @pl.when(step == 1)
        def _():
            second_pieces(1)

        make_terms(step + 2)
        for sub in range(PIECES):
            for way in range(2):
                sum_copy(step, way, sub).wait_recv()
                rows = slice(sub * piece, (sub + 1) * piece)
                total = sums[way, step + 1, rows, :].astype(jnp.float32) + terms[way, rows, :]
                sums[way, step + 1, rows, :] = total.astype(jnp.bfloat16)
                sum_copy(step + 1, way, sub).start()
        return carry

    lax.fori_loop(0, n_mp - 2, scatter_step, 0)
    second_pieces(2)
    make_terms(n_mp)
    for sub in range(PIECES):
        for way in range(2):
            sum_copy(n_mp - 2, way, sub).wait_recv()
            rows = slice(sub * piece, (sub + 1) * piece)
            total = sums[way, n_mp - 1, rows, :].astype(jnp.float32) + terms[way, rows, :]
            start = way * half + sub * piece
            out_ref[start:start + piece, :] = total.astype(jnp.bfloat16)

    def drain(step, carry):
        for way in range(2):
            for sub in range(SLICES):
                x_copy(step, way, sub).wait_send()
            for sub in range(PIECES):
                sum_copy(step, way, sub).wait_send()
        return carry

    lax.fori_loop(0, n_mp - 1, drain, 0)
    for sub in range(SLICES):
        for j in range(1, n_dp):
            token_copy(j, sub).wait_send()
    for w in range(kinds):
        for i in range(2 * groups - 1):
            weight_copy(w, me_dp, shard(w), i, partner).wait_send()


def local(
    pair_tokens,
    norm_gain,
    q_weight,
    k_weight,
    value_weight,
    o_weight,
    pair_row,
    pair_span,
    block_ids,
):
    dp_count = lax.axis_size("dp")
    mp_count = lax.axis_size("mp")
    own_index = lax.axis_index("dp")
    pairs_dev = pair_tokens.shape[0]
    pair_cap = pair_tokens.shape[1]
    width_local = pair_tokens.shape[2]
    all_pairs = pair_row.shape[0]
    most_sent = -(-pairs_dev // dp_count)
    tok_dev = block_ids.shape[0]
    rows_dev = tok_dev // ROW_TOKENS
    owners_all = (pair_row // rows_dev).reshape(dp_count, pairs_dev)
    same_owner = owners_all[:, :, None] == owners_all[:, None, :]
    listed = jnp.arange(pairs_dev)
    before = listed[None, :] < listed[:, None]
    rank_all = jnp.sum((same_owner & before[None]).astype(jnp.int32), axis=2)
    own_owner = lax.dynamic_index_in_dim(owners_all, own_index, 0, keepdims=False)
    own_rank = lax.dynamic_index_in_dim(rank_all, own_index, 0, keepdims=False)
    slots = jnp.arange(pair_cap, dtype=jnp.int32)
    sent = dp_count * most_sent
    own_slot = ((own_owner * most_sent + own_rank)[:, None] * pair_cap + slots[None, :]).reshape(-1)
    pick = (jnp.arange(sent * pair_cap)[:, None] == own_slot[None, :]).astype(jnp.bfloat16)
    outgoing = jnp.dot(
        pick,
        pair_tokens.reshape(pairs_dev * pair_cap, width_local),
        preferred_element_type=jnp.float32,
    ).astype(jnp.bfloat16)
    length = pair_span[:, 1] - pair_span[:, 0]
    source = jnp.arange(all_pairs, dtype=jnp.int32) // pairs_dev
    first = (pair_row % rows_dev) * ROW_TOKENS + pair_span[:, 0]
    place = source * most_sent + rank_all.reshape(-1)
    mine = owners_all.reshape(-1) == own_index
    match = (jnp.arange(sent)[:, None] == place[None, :]) & mine[None, :]
    first_of = jnp.sum(jnp.where(match, first[None, :], 0), axis=1)
    length_of = jnp.sum(jnp.where(match, length[None, :], 0), axis=1)
    placement_map = jnp.where(
        slots[None, :] < length_of[:, None], first_of[:, None] + slots[None, :], tok_dev
    ).reshape(-1)
    half = HEAD_SIZE // 2
    freq = 500000.0 ** (-(np.arange(half, dtype=np.float32) * 2.0 / HEAD_SIZE))
    freq = np.concatenate([freq, freq])[None, :].astype(np.float32)

    q_width = q_weight.shape[1]
    k_width = k_weight.shape[1]
    width = norm_gain.shape[0]
    far = dp_count - 1
    vmem = pl.BlockSpec(memory_space=pltpu.VMEM)
    anyspace = pl.BlockSpec(memory_space=pl.ANY)
    bf16 = jnp.bfloat16
    return pl.pallas_call(
        functools.partial(kernel, dp_count, mp_count),
        out_shape=jax.ShapeDtypeStruct((tok_dev, width_local), bf16),
        in_specs=[vmem, anyspace, vmem, anyspace, anyspace, anyspace, anyspace, vmem, vmem],
        out_specs=vmem,
        scratch_shapes=[
            pltpu.VMEM((sent * pair_cap, width_local), bf16),
            pltpu.VMEM((mp_count, tok_dev, width_local), bf16),
            pltpu.VMEM((width, q_width), bf16),
            pltpu.VMEM((width, k_width), bf16),
            pltpu.VMEM((width, k_width), bf16),
            pltpu.VMEM((o_weight.shape[0], width), bf16),
            pltpu.VMEM((tok_dev, q_width + 2 * k_width), jnp.float32),
            pltpu.VMEM((tok_dev, 1), jnp.float32),
            pltpu.VMEM((tok_dev, q_width), bf16),
            pltpu.VMEM((2, mp_count, tok_dev // 2, width_local), bf16),
            pltpu.VMEM((2, tok_dev // 2, width_local), jnp.float32),
            pltpu.VMEM((tok_dev, HEAD_SIZE), jnp.float32),
            pltpu.VMEM((tok_dev, HEAD_SIZE), jnp.float32),
            pltpu.VMEM((tok_dev, ROW_TOKENS), jnp.float32),
            pltpu.VMEM((tok_dev, sent * pair_cap), bf16),
            pltpu.SemaphoreType.DMA((5,)),
            pltpu.SemaphoreType.DMA((SLICES, far)),
            pltpu.SemaphoreType.DMA((SLICES, dp_count)),
            pltpu.SemaphoreType.DMA((5, far)),
            pltpu.SemaphoreType.DMA((5, dp_count)),
            pltpu.SemaphoreType.DMA((2, SLICES, mp_count - 1)),
            pltpu.SemaphoreType.DMA((2, SLICES, mp_count - 1)),
            pltpu.SemaphoreType.DMA((2, PIECES, mp_count - 1)),
            pltpu.SemaphoreType.DMA((2, PIECES, mp_count - 1)),
        ],
        compiler_params=pltpu.CompilerParams(
            collective_id=0, has_side_effects=True, vmem_limit_bytes=60 * 1024 * 1024
        ),
    )(
        placement_map[None, :],
        outgoing,
        norm_gain[None, :],
        q_weight,
        k_weight,
        value_weight,
        o_weight,
        block_ids.reshape(rows_dev, ROW_TOKENS),
        jnp.asarray(freq),
    )


def solution(mesh):
    placed = (
        P("dp", None, "mp"),
        P(),
        P("dp", "mp"),
        P("dp", "mp"),
        P("dp", "mp"),
        P("mp", "dp"),
        P(),
        P(),
        P("dp"),
    )
    return jax.shard_map(
        local, mesh=mesh, in_specs=placed, out_specs=P("dp", "mp"), check_vma=False
    )
```

```python
import functools

import jax
import jax.numpy as jnp
import numpy as np
from jax import lax
from jax.experimental import pallas as pl
from jax.experimental.pallas import tpu as pltpu
from jax.sharding import PartitionSpec as P

HEAD_SIZE = 128
ROW_TOKENS = 128
QUERY_PER_KV = 4
PIECES = 2
SLICES = 4
MESH = pl.DeviceIdType.MESH


def ring_member(place, count):
    place = lax.rem(place + 2 * count, count)
    return jnp.where(place < count // 2, 2 * place, 2 * (count - 1 - place) + 1)


def pieces_of_output(n_mp, width, chunk):
    if width != 2 * chunk:
        return 1
    order = list(range(0, n_mp, 2)) + list(range(1, n_mp, 2))[::-1]
    apart = all(order[p - 1] // 2 != order[(p + 1) % n_mp] // 2 for p in range(n_mp))
    return 2 if apart else 1


def kernel(
    n_dp, n_mp,
    map_ref, tok_ref, gain_ref, q_ref, k_ref, v_ref, o_ref, ids_ref, freq_ref,
    out_ref,
    xin, xg, wq, wk, wv, wo, acc, square, attn, sums, terms, cos_ref, sin_ref, vis_ref, put_ref,
    own_sem, t_send, t_recv, w_send, w_recv, x_send, x_recv, s_send, s_recv,
):
    me_dp = lax.axis_index("dp")
    me_mp = lax.axis_index("mp")

    def place_of(g):
        return jnp.where(lax.rem(g, 2) == 0, g // 2, n_mp - 1 - g // 2)

    place = place_of(me_mp)
    sides = (ring_member(place + 1, n_mp), ring_member(place - 1, n_mp))
    groups = n_dp // 2
    core = lax.rem(me_dp, 2)
    partner = me_dp + 1 - 2 * core
    others = [lax.rem(me_dp + 2 * j, n_dp) for j in range(1, groups)]
    tokens, chunk = out_ref.shape
    half = tokens // 2
    piece = half // PIECES
    block = tok_ref.shape[0] // n_dp
    width = o_ref.shape[1]
    n_out = pieces_of_output(n_mp, width, chunk)

    barrier = pltpu.get_barrier_semaphore()
    for side in sides:
        pl.semaphore_signal(barrier, inc=1, device_id={"mp": side}, device_id_type=MESH)
    for j in range(1, n_dp):
        peer = lax.rem(me_dp + j, n_dp)
        pl.semaphore_signal(barrier, inc=1, device_id={"dp": peer}, device_id_type=MESH)
    pl.semaphore_wait(barrier, 2 + n_dp - 1)

    def token_rows(owner):
        return pl.ds(pl.multiple_of(owner * block, 16), block)

    slice_width = chunk // SLICES

    def token_slice(sub):
        return pl.ds(sub * slice_width, slice_width)

    def token_copy(j, sub):
        peer = lax.rem(me_dp + j, n_dp)
        return pltpu.make_async_remote_copy(
            src_ref=tok_ref.at[token_rows(peer), token_slice(sub)],
            dst_ref=xin.at[token_rows(me_dp), token_slice(sub)],
            send_sem=t_send.at[sub, j - 1],
            recv_sem=t_recv.at[sub, me_dp],
            device_id={"dp": peer},
            device_id_type=MESH,
        )

    def token_arrival(j, sub):
        peer = lax.rem(me_dp + j, n_dp)
        return pltpu.make_async_remote_copy(
            src_ref=tok_ref.at[token_rows(peer), token_slice(sub)],
            dst_ref=xin.at[token_rows(peer), token_slice(sub)],
            send_sem=t_send.at[sub, j - 1],
            recv_sem=t_recv.at[sub, peer],
            device_id={"dp": peer},
            device_id_type=MESH,
        )

    own_tokens = pltpu.make_async_copy(
        tok_ref.at[token_rows(me_dp), :], xin.at[token_rows(me_dp), :], own_sem.at[4]
    )
    for sub in range(SLICES):
        for j in range(1, n_dp):
            token_copy(j, sub).start()
    own_tokens.start()

    def hop_of(g):
        gap = lax.rem(place_of(g) - place + n_mp, n_mp)
        gap = jnp.where(gap == 0, n_mp, gap)
        return jnp.minimum(gap, jnp.where(gap == n_mp, n_mp, n_mp - gap))

    def out_columns(which, owner):
        if n_out == 1:
            return owner * 0
        later = (hop_of(2 * owner + 1) < hop_of(2 * owner)).astype(jnp.int32)
        return chunk * (later if which == 3 else 1 - later)

    def part(which, owner):
        if which >= 3:
            start = owner * width + out_columns(which, owner)
            return wo.at[:, pl.ds(pl.multiple_of(start, 128), width // n_out)]
        full = (wq, wk, wv)[which]
        depth = q_ref.shape[0]
        return full.at[pl.ds(pl.multiple_of(owner * depth, 16), depth), :]

    def shard(which):
        if which >= 3:
            start = out_columns(which, me_dp)
            return o_ref.at[:, pl.ds(pl.multiple_of(start, 128), width // n_out)]
        return (q_ref, k_ref, v_ref)[which]

    kinds = 3 + n_out

    def weight_copy(which, owner, source, slot, peer):
        return pltpu.make_async_remote_copy(
            src_ref=source,
            dst_ref=part(which, owner),
            send_sem=w_send.at[which, slot],
            recv_sem=w_recv.at[which, owner],
            device_id={"dp": peer},
            device_id_type=MESH,
        )

    def x_copy(step, way, sub):
        sign = -1 if way == 0 else 1
        chunk_of = ring_member(place + sign * step, n_mp)
        ref = xg.at[chunk_of, pl.ds(way * half, half), token_slice(sub)]
        return pltpu.make_async_remote_copy(
            src_ref=ref,
            dst_ref=ref,
            send_sem=x_send.at[way, sub, step],
            recv_sem=x_recv.at[way, sub, step],
            device_id={"mp": sides[way]},
            device_id_type=MESH,
        )

    def x_arrival(step, way, sub):
        sign = -1 if way == 0 else 1
        chunk_of = ring_member(place + sign * (step + 1), n_mp)
        ref = xg.at[chunk_of, pl.ds(way * half, half), token_slice(sub)]
        return pltpu.make_async_remote_copy(
            src_ref=ref,
            dst_ref=ref,
            send_sem=x_send.at[way, sub, step],
            recv_sem=x_recv.at[way, sub, step],
            device_id={"mp": sides[way]},
            device_id_type=MESH,
        )

    owns = [
        pltpu.make_async_copy(
            (q_ref, k_ref, v_ref)[w],
            part(w, me_dp),
            own_sem.at[w],
        )
        for w in range(3)
    ]
    owns.append(
        pltpu.make_async_copy(
            o_ref,
            wo.at[:, pl.ds(pl.multiple_of(me_dp * width, 128), width)],
            own_sem.at[3],
        )
    )
    def second_chunk(owner):
        return (owner * width + out_columns(4, owner)) // chunk

    def second_stage(owner):
        hop = hop_of(second_chunk(owner))
        return jnp.where(hop == n_mp, 2, jnp.where(hop > 2, 1, 0))

    held = second_stage(me_dp) == 2

    def send_second():
        for j, peer in enumerate(others):
            weight_copy(4, me_dp, shard(4), 1 + j, peer).start()

    for w in range(3):
        for j, peer in enumerate(others):
            weight_copy(w, me_dp, shard(w), 1 + j, peer).start()
    for w in range(3):
        owns[w].start()
        weight_copy(w, me_dp, shard(w), 0, partner).start()

    def tables(r, carry):
        rows = pl.ds(pl.multiple_of(r * ROW_TOKENS, ROW_TOKENS), ROW_TOKENS)
        ids_j = jnp.broadcast_to(ids_ref[pl.ds(r, 1), :], (ROW_TOKENS, ROW_TOKENS)).astype(
            jnp.float32
        )
        ids_i = jnp.transpose(ids_j)
        pair_i = jnp.floor((ids_i + 0.5) * (1.0 / 3.0))
        pair_j = jnp.floor((ids_j + 0.5) * (1.0 / 3.0))
        at_i = lax.broadcasted_iota(jnp.int32, (ROW_TOKENS, ROW_TOKENS), 0)
        at_j = lax.broadcasted_iota(jnp.int32, (ROW_TOKENS, ROW_TOKENS), 1)
        hidden = (ids_i - 3.0 * pair_i == 2.0) & (ids_j - 3.0 * pair_j == 1.0)
        seen = jnp.where((at_j <= at_i) & (pair_i == pair_j), 1.0, 0.0)
        seen = jnp.where(hidden, 0.0, seen)
        vis_ref[rows, :] = seen
        angle = (jnp.sum(seen, axis=1, keepdims=True) - 1.0) * freq_ref[...]
        lane = lax.broadcasted_iota(jnp.int32, (ROW_TOKENS, HEAD_SIZE), 1)
        sine = jnp.sin(angle)
        cos_ref[rows, :] = jnp.cos(angle)
        sin_ref[rows, :] = jnp.where(lane < HEAD_SIZE // 2, -sine, sine)
        return carry

    lax.fori_loop(0, tokens // ROW_TOKENS, tables, 0)
    acc[...] = jnp.zeros_like(acc)
    square[...] = jnp.zeros_like(square)

    own_tokens.wait()
    at = lax.broadcasted_iota(jnp.int32, (tokens, n_dp * block), 0)
    put_ref[...] = jnp.where(at == map_ref[...], 1.0, 0.0).astype(jnp.bfloat16)
    for sub in range(SLICES):
        for j in range(1, n_dp):
            token_arrival(j, sub).wait_recv()
        columns = slice(sub * slice_width, (sub + 1) * slice_width)
        xg[me_mp, :, columns] = jnp.dot(
            put_ref[...], xin[:, columns], preferred_element_type=jnp.float32
        ).astype(jnp.bfloat16)
        for way in range(2):
            x_copy(0, way, sub).start()
    owns[3].start()
    for w in range(3, kinds):
        weight_copy(w, me_dp, shard(w), 0, partner).start()

    def pass_weight(w):
        for j in range(1, groups):
            owner = lax.rem(me_dp + n_dp - 2 * j, n_dp)
            weight_copy(w, owner, part(w, owner), 0, partner).wait_recv()
            weight_copy(w, owner, part(w, owner), groups + j - 1, partner).start()

    def weight_done(w):
        for i in range(groups):
            owner = lax.rem(partner + 2 * i, n_dp)
            weight_copy(w, owner, part(w, owner), 0, partner).wait_recv()

    q_width = wq.shape[1]
    k_width = wk.shape[1]

    def project(way, g):
        halves = pl.ds(pl.multiple_of(way * half, 16), half)
        wide = xg[g, halves, :].astype(jnp.float32)
        square[halves, :] += jnp.sum(wide * wide, axis=1, keepdims=True)
        columns = pl.ds(pl.multiple_of(g * chunk, 128), chunk)
        scaled = (wide * gain_ref[:, columns]).astype(jnp.bfloat16)
        rows = pl.ds(pl.multiple_of(g * chunk, 16), chunk)
        acc[halves, 0:q_width] += jnp.dot(
            scaled, wq[rows, :], preferred_element_type=jnp.float32
        )
        acc[halves, q_width:q_width + k_width] += jnp.dot(
            scaled, wk[rows, :], preferred_element_type=jnp.float32
        )
        acc[halves, q_width + k_width:] += jnp.dot(
            scaled, wv[rows, :], preferred_element_type=jnp.float32
        )

    def project_step(hop, near):
        def one(way, carry):
            g = ring_member(place + jnp.where(way == 0, -hop, hop), n_mp)
            is_near = (g * chunk) // (2 * q_ref.shape[0]) == me_dp // 2

            @pl.when(is_near == near)
            def _():
                project(way, g)

            return carry

        lax.fori_loop(0, 2, one, 0)

    for w in range(3):
        owns[w].wait()
        owner = partner
        weight_copy(w, owner, part(w, owner), 0, partner).wait_recv()

    def gather_step(step, carry):
        project_step(step, True)
        for sub in range(SLICES):
            for way in range(2):
                x_arrival(step, way, sub).wait_recv()
                x_copy(step + 1, way, sub).start()
        return carry

    def weight_rest(w):
        for i in range(1, groups):
            owner = lax.rem(partner + 2 * i, n_dp)
            weight_copy(w, owner, part(w, owner), 0, partner).wait_recv()

    late = max(n_mp - 3, 0)
    lax.fori_loop(0, late, gather_step, 0)
    pass_weight(0)
    lax.fori_loop(late, n_mp - 2, gather_step, 0)
    pass_weight(1)
    pass_weight(2)
    for j, peer in enumerate(others):
        weight_copy(3, me_dp, shard(3), 1 + j, peer).start()
    project_step(n_mp - 2, True)
    for w in range(3):
        weight_rest(w)

    def project_far(hop, carry):
        project_step(hop, False)
        return carry

    lax.fori_loop(0, n_mp - 1, project_far, 0)
    for sub in range(SLICES):
        for way in range(2):
            x_arrival(n_mp - 2, way, sub).wait_recv()

    def project_last(way, carry):
        project(way, ring_member(place + jnp.where(way == 0, 1 - n_mp, n_mp - 1), n_mp))
        return carry

    lax.fori_loop(0, 2, project_last, 0)
    acc[...] = acc[...] * lax.rsqrt(square[...] / (n_mp * chunk) + 1e-05)

    def turn(u, cosine, sine):
        return (u * cosine + pltpu.roll(u, HEAD_SIZE // 2, 1) * sine).astype(jnp.bfloat16)

    def attend(r, carry):
        rows = pl.ds(pl.multiple_of(r * ROW_TOKENS, ROW_TOKENS), ROW_TOKENS)
        cosine = cos_ref[rows, :]
        sine = sin_ref[rows, :]
        seen = vis_ref[rows, :] > 0.5
        for kv in range(k_width // HEAD_SIZE):
            at_k = q_width + kv * HEAD_SIZE
            key = turn(acc[rows, at_k:at_k + HEAD_SIZE], cosine, sine)
            value = acc[rows, at_k + k_width:at_k + k_width + HEAD_SIZE].astype(jnp.bfloat16)
            for h in range(kv * QUERY_PER_KV, (kv + 1) * QUERY_PER_KV):
                at = slice(h * HEAD_SIZE, (h + 1) * HEAD_SIZE)
                query = turn(acc[rows, at], cosine, sine)
                scores = lax.dot_general(
                    query, key, (((1,), (1,)), ((), ())), preferred_element_type=jnp.float32
                ) * HEAD_SIZE ** (-0.5)
                scores = jnp.where(seen, scores, -1e30)
                expo = jnp.exp(scores - jnp.max(scores, axis=-1, keepdims=True))
                probs = (expo / jnp.sum(expo, axis=-1, keepdims=True)).astype(jnp.bfloat16)
                attn[rows, at] = jnp.dot(
                    probs, value, preferred_element_type=jnp.float32
                ).astype(jnp.bfloat16)
        return carry

    lax.fori_loop(0, tokens // ROW_TOKENS, attend, 0)
    owns[3].wait()
    pass_weight(3)
    if kinds == 5:
        pl.when(jnp.logical_not(held))(send_second)
    weight_done(3)

    def make_terms(hop):
        for way in range(2):
            sign = -1 if way == 0 else 1
            g = ring_member(place + sign * hop, n_mp)
            columns = pl.ds(pl.multiple_of(g * chunk, 128), chunk)
            terms[way] = jnp.dot(
                attn[way * half:(way + 1) * half, :],
                wo[:, columns],
                preferred_element_type=jnp.float32,
            )

    def sum_copy(slot, way, sub):
        rows = pl.ds(sub * piece, piece)
        return pltpu.make_async_remote_copy(
            src_ref=sums.at[way, slot, rows, :],
            dst_ref=sums.at[way, slot + 1, rows, :],
            send_sem=s_send.at[way, sub, slot],
            recv_sem=s_recv.at[way, sub, slot],
            device_id={"mp": sides[way]},
            device_id_type=MESH,
        )

    make_terms(1)
    for sub in range(PIECES):
        for way in range(2):
            rows = slice(sub * piece, (sub + 1) * piece)
            sums[way, 0, rows, :] = terms[way, rows, :].astype(jnp.bfloat16)
            sum_copy(0, way, sub).start()

    def second_pieces(stage):
        if kinds < 5:
            return
        for j in range(1, groups):
            owner = lax.rem(me_dp + n_dp - 2 * j, n_dp)

            @pl.when(second_stage(owner) == stage)
            def _():
                weight_copy(4, owner, part(4, owner), 0, partner).wait_recv()
                weight_copy(4, owner, part(4, owner), groups + j - 1, partner).start()

        for i in range(groups):
            owner = lax.rem(partner + 2 * i, n_dp)

            @pl.when(second_stage(owner) == stage)
            def _():
                weight_copy(4, owner, part(4, owner), 0, partner).wait_recv()

    second_pieces(0)
    if kinds == 5:
        pl.when(held)(send_second)

    def scatter_step(step, carry):
        @pl.when(step == 1)
        def _():
            second_pieces(1)

        make_terms(step + 2)
        for sub in range(PIECES):
            for way in range(2):
                sum_copy(step, way, sub).wait_recv()
                rows = slice(sub * piece, (sub + 1) * piece)
                total = sums[way, step + 1, rows, :].astype(jnp.float32) + terms[way, rows, :]
                sums[way, step + 1, rows, :] = total.astype(jnp.bfloat16)
                sum_copy(step + 1, way, sub).start()
        return carry

    lax.fori_loop(0, n_mp - 2, scatter_step, 0)
    second_pieces(2)
    make_terms(n_mp)
    for sub in range(PIECES):
        for way in range(2):
            sum_copy(n_mp - 2, way, sub).wait_recv()
            rows = slice(sub * piece, (sub + 1) * piece)
            total = sums[way, n_mp - 1, rows, :].astype(jnp.float32) + terms[way, rows, :]
            start = way * half + sub * piece
            out_ref[start:start + piece, :] = total.astype(jnp.bfloat16)

    def drain(step, carry):
        for way in range(2):
            for sub in range(SLICES):
                x_copy(step, way, sub).wait_send()
            for sub in range(PIECES):
                sum_copy(step, way, sub).wait_send()
        return carry

    lax.fori_loop(0, n_mp - 1, drain, 0)
    for sub in range(SLICES):
        for j in range(1, n_dp):
            token_copy(j, sub).wait_send()
    for w in range(kinds):
        for i in range(2 * groups - 1):
            weight_copy(w, me_dp, shard(w), i, partner).wait_send()


def local(
    pair_tokens,
    norm_gain,
    q_weight,
    k_weight,
    value_weight,
    o_weight,
    pair_row,
    pair_span,
    block_ids,
):
    dp_count = lax.axis_size("dp")
    mp_count = lax.axis_size("mp")
    own_index = lax.axis_index("dp")
    pairs_dev = pair_tokens.shape[0]
    pair_cap = pair_tokens.shape[1]
    width_local = pair_tokens.shape[2]
    all_pairs = pair_row.shape[0]
    most_sent = -(-pairs_dev // dp_count)
    tok_dev = block_ids.shape[0]
    rows_dev = tok_dev // ROW_TOKENS
    owners_all = (pair_row // rows_dev).reshape(dp_count, pairs_dev)
    same_owner = owners_all[:, :, None] == owners_all[:, None, :]
    listed = jnp.arange(pairs_dev)
    before = listed[None, :] < listed[:, None]
    rank_all = jnp.sum((same_owner & before[None]).astype(jnp.int32), axis=2)
    own_owner = lax.dynamic_index_in_dim(owners_all, own_index, 0, keepdims=False)
    own_rank = lax.dynamic_index_in_dim(rank_all, own_index, 0, keepdims=False)
    slots = jnp.arange(pair_cap, dtype=jnp.int32)
    sent = dp_count * most_sent
    own_slot = ((own_owner * most_sent + own_rank)[:, None] * pair_cap + slots[None, :]).reshape(-1)
    pick = (jnp.arange(sent * pair_cap)[:, None] == own_slot[None, :]).astype(jnp.bfloat16)
    outgoing = jnp.dot(
        pick,
        pair_tokens.reshape(pairs_dev * pair_cap, width_local),
        preferred_element_type=jnp.float32,
    ).astype(jnp.bfloat16)
    length = pair_span[:, 1] - pair_span[:, 0]
    source = jnp.arange(all_pairs, dtype=jnp.int32) // pairs_dev
    first = (pair_row % rows_dev) * ROW_TOKENS + pair_span[:, 0]
    place = source * most_sent + rank_all.reshape(-1)
    mine = owners_all.reshape(-1) == own_index
    match = (jnp.arange(sent)[:, None] == place[None, :]) & mine[None, :]
    first_of = jnp.sum(jnp.where(match, first[None, :], 0), axis=1)
    length_of = jnp.sum(jnp.where(match, length[None, :], 0), axis=1)
    placement_map = jnp.where(
        slots[None, :] < length_of[:, None], first_of[:, None] + slots[None, :], tok_dev
    ).reshape(-1)
    half = HEAD_SIZE // 2
    freq = 500000.0 ** (-(np.arange(half, dtype=np.float32) * 2.0 / HEAD_SIZE))
    freq = np.concatenate([freq, freq])[None, :].astype(np.float32)

    q_width = q_weight.shape[1]
    k_width = k_weight.shape[1]
    width = norm_gain.shape[0]
    far = dp_count - 1
    vmem = pl.BlockSpec(memory_space=pltpu.VMEM)
    anyspace = pl.BlockSpec(memory_space=pl.ANY)
    bf16 = jnp.bfloat16
    return pl.pallas_call(
        functools.partial(kernel, dp_count, mp_count),
        out_shape=jax.ShapeDtypeStruct((tok_dev, width_local), bf16),
        in_specs=[vmem, anyspace, vmem, anyspace, anyspace, anyspace, anyspace, vmem, vmem],
        out_specs=vmem,
        scratch_shapes=[
            pltpu.VMEM((sent * pair_cap, width_local), bf16),
            pltpu.VMEM((mp_count, tok_dev, width_local), bf16),
            pltpu.VMEM((width, q_width), bf16),
            pltpu.VMEM((width, k_width), bf16),
            pltpu.VMEM((width, k_width), bf16),
            pltpu.VMEM((o_weight.shape[0], width), bf16),
            pltpu.VMEM((tok_dev, q_width + 2 * k_width), jnp.float32),
            pltpu.VMEM((tok_dev, 1), jnp.float32),
            pltpu.VMEM((tok_dev, q_width), bf16),
            pltpu.VMEM((2, mp_count, tok_dev // 2, width_local), bf16),
            pltpu.VMEM((2, tok_dev // 2, width_local), jnp.float32),
            pltpu.VMEM((tok_dev, HEAD_SIZE), jnp.float32),
            pltpu.VMEM((tok_dev, HEAD_SIZE), jnp.float32),
            pltpu.VMEM((tok_dev, ROW_TOKENS), jnp.float32),
            pltpu.VMEM((tok_dev, sent * pair_cap), bf16),
            pltpu.SemaphoreType.DMA((5,)),
            pltpu.SemaphoreType.DMA((SLICES, far)),
            pltpu.SemaphoreType.DMA((SLICES, dp_count)),
            pltpu.SemaphoreType.DMA((5, far)),
            pltpu.SemaphoreType.DMA((5, dp_count)),
            pltpu.SemaphoreType.DMA((2, SLICES, mp_count - 1)),
            pltpu.SemaphoreType.DMA((2, SLICES, mp_count - 1)),
            pltpu.SemaphoreType.DMA((2, PIECES, mp_count - 1)),
            pltpu.SemaphoreType.DMA((2, PIECES, mp_count - 1)),
        ],
        compiler_params=pltpu.CompilerParams(
            collective_id=0, has_side_effects=True, vmem_limit_bytes=60 * 1024 * 1024
        ),
    )(
        placement_map[None, :],
        outgoing,
        norm_gain[None, :],
        q_weight,
        k_weight,
        value_weight,
        o_weight,
        block_ids.reshape(rows_dev, ROW_TOKENS),
        jnp.asarray(freq),
    )


def solution(mesh):
    placed = (
        P("dp", None, "mp"),
        P(),
        P("dp", "mp"),
        P("dp", "mp"),
        P("dp", "mp"),
        P("mp", "dp"),
        P(),
        P(),
        P("dp"),
    )
    return jax.shard_map(
        local, mesh=mesh, in_specs=placed, out_specs=P("dp", "mp"), check_vma=False
    )
```
